32 devices in a mesh: groups: 2 (over y), wide: 8 (over z, x), short: 2 (over core).
Axes of the slice: x: 2, y: 2, z: 4, core: 2. Of those that a mesh axis runs over, the one named last changes fastest.
Arguments:
- tokens: bfloat16 [64, 5120], P(('groups', 'wide'), 'short'), parts along dimension 0, may hold values from -6 to 6
- norm_gain: float32 [5120], P('short'), may hold values from 0.5 to 1.5
- mixer_in: bfloat16 [5120, 2, 5888], P('short', None, 'wide'), may hold values from -0.078125 to 0.078125
- shared_in: bfloat16 [5120, 512], P('short', 'wide'), may hold values from -0.078125 to 0.078125
- step_in: bfloat16 [5120, 32], P('short'), may hold values from -0.078125 to 0.078125
- step_bias: float32 [32], P('short'), may hold values from -2 to 1
- decay_rate: float32 [32], P('short'), may hold values from 0.05 to 4
- skip_gain: float32 [32], P('short'), may hold values from 0.2 to 1.5
- cached_keys: bfloat16 [16, 512, 512], P(('groups', 'wide'), None, 'short'), parts along dimension 0, may hold values from -64 to 64
- cached_values: bfloat16 [16, 512, 512], P(('groups', 'wide'), None, 'short'), parts along dimension 0, may hold values from -6 to 6
- lengths: int32 [16], P(('groups', 'wide')), parts along dimension 0, may hold values from 2 to 512, as said below
- state_cache: bfloat16 [16, 32, 128, 256], P(('groups', 'wide'), 'short'), parts along dimension 0, may hold values from -6 to 6
- mixer_gain: float32 [4096], P('short'), may hold values from 0.5 to 1.5
- mixer_out: bfloat16 [2, 3328, 5120], P(None, 'wide', 'short'), may hold values from -0.078125 to 0.078125
- gate_weight: bfloat16 [5120, 21504], P('short', 'wide'), may hold values from -0.078125 to 0.078125
- up_weight: bfloat16 [5120, 21504], P('short', 'wide'), may hold values from -0.078125 to 0.078125
- down_weight: bfloat16 [21504, 5120], P('wide', 'short'), may hold values from -0.0390625 to 0.0390625
Outputs:
- mixed: bfloat16 [64, 5120], P(('groups', 'wide'), 'short'), parts along dimension 0
The draws below stay inside these ranges and needn't reach their ends.
There are 2 independent parts, one for each index of `groups`. The reference program is written for one: setup_inputs(seed, part) draws one part's arguments, and reference() takes and returns one part's arrays. A program takes and returns all parts, laid end to end along the dimension named above; an argument that names none is the same for every part. Nothing has to cross between parts.
Inputs may be any that keep to these rules, and one draw needn't show every extreme that they name: `lengths`: in every draw some request holds exactly 512 earlier tokens.
All inputs are finite; a program needn't handle non-finite values.
Results may differ from the reference program's by a relative error of at most 0.009.
Values may be sent and summed in bfloat16 or wider, within the bound.
A program may use at most 128 MiB of HBM per device.

```python
import math
import jax
import jax.numpy as jnp
from jax import lax

D = 5120
QUERY_HEADS = 20
KEY_VALUE_HEADS = 4
HEAD_SIZE = 128
MH = 32
MP = 128
NS = 256
FF = 21504
CACHE_SLOTS = 512
DRAFT_TOKENS = 4
HEAD_GROUPS = 2
REQUEST_COUNT = 8
ROWS = 32
GCOL = 5888
OCOL = 3328


def draw_lengths(key, part):
    drawn = jax.random.randint(key, (REQUEST_COUNT,), 2, CACHE_SLOTS + 1)
    chosen = jax.random.randint(jax.random.fold_in(key, 11), (), 0, REQUEST_COUNT)
    return jnp.where(jnp.arange(REQUEST_COUNT) == chosen, CACHE_SLOTS, drawn).astype(jnp.int32)


def draw_cached_keys(key, part):
    cache_entries = jax.random.normal(key, (REQUEST_COUNT, CACHE_SLOTS, KEY_VALUE_HEADS * HEAD_SIZE), jnp.float32)
    return jnp.clip(cache_entries, -64.0, 64.0).astype(jnp.bfloat16)


def block_levels(key, extent, shards, smallest, top_value):
    def one(axis_at, blocks):
        draws = jax.random.uniform(jax.random.fold_in(jax.random.fold_in(key, 6), axis_at), (blocks,), jnp.float32, smallest / len(shards), top_value / len(shards))
        return jnp.repeat(jnp.exp(draws), extent[axis_at] // blocks).reshape((-1,) + (1,) * (len(extent) - axis_at - 1))

    level = one(*shards[0])
    for cut in shards[1:]:
        level = level * one(*cut)
    return level


def normal_values(key, shape, spread, bound, cuts=(), kind=jnp.bfloat16):
    result = jax.random.normal(key, shape, jnp.float32) * spread
    if len(cuts) > 0:
        result = block_levels(key, shape, cuts, -0.22, 0.18) * result
    return jnp.clip(result, min=-bound, max=bound).astype(kind)


def setup_inputs(seed: int = 0, part: int = 0) -> dict:
    key_list = jax.random.split(jax.random.key(seed), 18)
    part_splits = jax.random.split(jax.random.fold_in(key_list[17], part), 18)
    return {
        "tokens": normal_values(part_splits[0], (ROWS, D), 1.0, 6.0, ((0, 8), (1, 2))),
        "norm_gain": jnp.clip(1.0 + 0.1 * jax.random.normal(key_list[1], (D,), jnp.float32), 0.5, 1.5),
        "mixer_in": normal_values(key_list[2], (D, HEAD_GROUPS, GCOL), D ** -0.5, 0.078125, ((0, 2), (2, 8))),
        "shared_in": normal_values(key_list[3], (D, 2 * NS), D ** -0.5, 0.078125, ((0, 2), (1, 8))),
        "step_in": normal_values(key_list[4], (D, MH), D ** -0.5, 0.078125, ((0, 2),)),
        "step_bias": jnp.clip(-2.0 + 3.0 * jax.random.uniform(key_list[5], (MH,), jnp.float32) ** block_levels(key_list[5], (MH,), ((0, 2),), -0.2, 0.2), -2.0, 1.0),
        "decay_rate": jnp.clip(jnp.exp(math.log(4.0) - 4.3820266 * jax.random.uniform(key_list[6], (MH,), jnp.float32) ** block_levels(key_list[6], (MH,), ((0, 2),), -0.2, 0.2)), 0.05, 4.0),
        "skip_gain": jnp.clip(0.2 + 1.3 * jax.random.uniform(key_list[7], (MH,), jnp.float32) ** block_levels(key_list[7], (MH,), ((0, 2),), -0.2, 0.2), 0.2, 1.5),
        "cached_keys": draw_cached_keys(jax.random.fold_in(jax.random.fold_in(key_list[17], part), 71), part),
        "cached_values": normal_values(part_splits[9], (REQUEST_COUNT, CACHE_SLOTS, KEY_VALUE_HEADS * HEAD_SIZE), 1.0, 6.0, ((0, 8), (2, 2))),
        "lengths": draw_lengths(jax.random.fold_in(jax.random.fold_in(key_list[17], part), 71), part),
        "state_cache": normal_values(part_splits[11], (REQUEST_COUNT, MH, MP, NS), 1.0, 6.0, ((0, 8), (1, 2))),
        "mixer_gain": jnp.clip(1.0 + 0.1 * jax.random.normal(key_list[12], (MH * MP,), jnp.float32), 0.5, 1.5),
        "mixer_out": normal_values(key_list[13], (HEAD_GROUPS, OCOL, D), (HEAD_GROUPS * OCOL) ** -0.5, 0.078125, ((1, 8), (2, 2))),
        "gate_weight": normal_values(key_list[14], (D, FF), D ** -0.5, 0.078125, ((0, 2), (1, 8))),
        "up_weight": normal_values(key_list[15], (D, FF), D ** -0.5, 0.078125, ((0, 2), (1, 8))),
        "down_weight": normal_values(key_list[16], (FF, D), FF ** -0.5, 0.0390625, ((0, 8), (1, 2))),
    }


epsilon = 1e-05

def rotate(vectors, cos_table, sin_table):
    half_width = vectors.shape[-1] // 2
    first_half = vectors[..., :half_width]
    second_half = vectors[..., half_width:]
    return jnp.concatenate([first_half * cos_table - second_half * sin_table, second_half * cos_table + first_half * sin_table], axis=-1)

def rope_tables(positions):
    frequency = 10000.0 ** (-(jnp.arange(HEAD_SIZE // 2, dtype=jnp.float32) * 2.0 / HEAD_SIZE))
    angles = positions.astype(jnp.float32)[..., None] * frequency
    return (jnp.cos(angles), jnp.sin(angles))

def attend_one(packed):
    queries, fresh_keys, fresh_values, key_tile_block, value_tile_block, length = packed
    score_scale = HEAD_SIZE ** (-0.5)
    query_float = queries.astype(jnp.float32)
    scores_cache = jnp.einsum('tkgd,pkd->kgtp', query_float, key_tile_block.astype(jnp.float32)) * score_scale
    scores_new = jnp.einsum('tkgd,ukd->kgtu', query_float, fresh_keys.astype(jnp.float32)) * score_scale
    live_keys = jnp.arange(key_tile_block.shape[0], dtype=jnp.int32) < length
    causal = jnp.arange(DRAFT_TOKENS)[None, :] <= jnp.arange(DRAFT_TOKENS)[:, None]
    scores_cache = jnp.where(live_keys, scores_cache, -1e+30)
    scores_new = jnp.where(causal, scores_new, -1e+30)
    highest = jnp.maximum(lax.optimization_barrier(jnp.max(scores_cache, axis=-1)), lax.optimization_barrier(jnp.max(scores_new, axis=-1)))[..., None]
    weight_cache = jnp.exp(scores_cache - highest)
    weight_new = jnp.exp(scores_new - highest)
    denominator = lax.optimization_barrier(jnp.sum(weight_cache, axis=-1, keepdims=True)) + lax.optimization_barrier(jnp.sum(weight_new, axis=-1, keepdims=True))
    probs_cache = (weight_cache / denominator).astype(jnp.bfloat16)
    probs_new = (weight_new / denominator).astype(jnp.bfloat16)
    attended = jnp.einsum('kgtp,pkd->tkgd', probs_cache.astype(jnp.float32), value_tile_block.astype(jnp.float32))
    attended = attended + jnp.einsum('kgtu,ukd->tkgd', probs_new.astype(jnp.float32), fresh_values.astype(jnp.float32))
    return attended.astype(jnp.bfloat16)

def scan_one(state_block, inputs_x, gates_z, b_vals, c_vals, step_sizes, decay_rates, skip_gain, head_gain):
    hstate = state_block.astype(jnp.float32)
    in_active = jax.nn.silu(inputs_x.astype(jnp.float32))
    write_vec = jax.nn.silu(b_vals.astype(jnp.float32))
    read_vec = jax.nn.silu(c_vals.astype(jnp.float32))
    outputs = []
    for draft_index in range(DRAFT_TOKENS):
        decays = jnp.exp(-step_sizes[draft_index] * decay_rates)
        inject = (step_sizes[draft_index][:, None] * in_active[draft_index])[:, :, None] * write_vec[draft_index][None, None, :]
        hstate = decays[:, None, None] * hstate + inject
        readout = jnp.einsum('hpn,n->hp', hstate, read_vec[draft_index], precision=lax.Precision.HIGHEST)
        outputs.append(readout + skip_gain[:, None] * in_active[draft_index])
    gated = jnp.stack(outputs) * jax.nn.silu(gates_z.astype(jnp.float32))
    mean_square = lax.optimization_barrier(jnp.mean(gated * gated, axis=-1, keepdims=True))
    return (gated * lax.rsqrt(mean_square + epsilon) * head_gain).astype(jnp.bfloat16)

def reference(tokens, norm_gain, mixer_in, shared_in, step_in, step_bias, decay_rate, skip_gain, cached_keys, cached_values, lengths, state_cache, mixer_gain, mixer_out, gate_weight, up_weight, down_weight):
    q_heads = QUERY_HEADS // HEAD_GROUPS
    key_value_heads = KEY_VALUE_HEADS // HEAD_GROUPS
    ssm_heads = MH // HEAD_GROUPS
    repeat_factor = QUERY_HEADS // KEY_VALUE_HEADS
    query_size = q_heads * HEAD_SIZE
    key_size = key_value_heads * HEAD_SIZE
    m_size = ssm_heads * MP
    rows_float = tokens.astype(jnp.float32)
    inv_rms = lax.rsqrt(lax.optimization_barrier(jnp.mean(rows_float * rows_float, axis=1, keepdims=True)) + epsilon)
    normed = (rows_float * inv_rms * norm_gain[None, :]).astype(jnp.bfloat16)
    grouped_heads = jnp.dot(normed, mixer_in.reshape(D, HEAD_GROUPS * GCOL), preferred_element_type=jnp.float32).astype(jnp.bfloat16)
    grouped_heads = grouped_heads.reshape(ROWS, HEAD_GROUPS, GCOL)
    shared = jnp.dot(normed, shared_in, preferred_element_type=jnp.float32).astype(jnp.bfloat16)
    step_raw = jnp.dot(normed, step_in, preferred_element_type=jnp.float32)
    gate_sum = jnp.dot(normed, gate_weight, preferred_element_type=jnp.float32)
    up_sum = jnp.dot(normed, up_weight, preferred_element_type=jnp.float32)
    hidden = (jax.nn.silu(gate_sum) * up_sum).astype(jnp.bfloat16)
    queries = grouped_heads[:, :, :query_size].reshape(REQUEST_COUNT, DRAFT_TOKENS, QUERY_HEADS, HEAD_SIZE)
    fresh_keys = grouped_heads[:, :, query_size:query_size + key_size].reshape(REQUEST_COUNT, DRAFT_TOKENS, KEY_VALUE_HEADS, HEAD_SIZE)
    fresh_values = grouped_heads[:, :, query_size + key_size:query_size + 2 * key_size].reshape(REQUEST_COUNT, DRAFT_TOKENS, KEY_VALUE_HEADS, HEAD_SIZE)
    x_start = query_size + 2 * key_size
    inputs_x = grouped_heads[:, :, x_start:x_start + m_size].reshape(REQUEST_COUNT, DRAFT_TOKENS, MH, MP)
    gates_z = grouped_heads[:, :, x_start + m_size:x_start + 2 * m_size].reshape(REQUEST_COUNT, DRAFT_TOKENS, MH, MP)
    positions = lengths[:, None] + jnp.arange(DRAFT_TOKENS, dtype=jnp.int32)[None, :]
    cos_table, sin_table = rope_tables(positions)
    cos_table = cos_table[:, :, None, :]
    sin_table = sin_table[:, :, None, :]
    rotated_queries = rotate(queries.astype(jnp.float32), cos_table, sin_table).astype(jnp.bfloat16)
    keys_rot = rotate(fresh_keys.astype(jnp.float32), cos_table, sin_table).astype(jnp.bfloat16)
    rotated_queries = rotated_queries.reshape(REQUEST_COUNT, DRAFT_TOKENS, KEY_VALUE_HEADS, repeat_factor, HEAD_SIZE)
    key_tile_block = cached_keys.reshape(REQUEST_COUNT, CACHE_SLOTS, KEY_VALUE_HEADS, HEAD_SIZE)
    value_tile_block = cached_values.reshape(REQUEST_COUNT, CACHE_SLOTS, KEY_VALUE_HEADS, HEAD_SIZE)
    attention = lax.map(attend_one, (rotated_queries, keys_rot, fresh_values, key_tile_block, value_tile_block, lengths))
    step_sizes = jax.nn.softplus(step_raw.reshape(REQUEST_COUNT, DRAFT_TOKENS, MH) + step_bias[None, None, :])
    b_vals = shared[:, :NS].reshape(REQUEST_COUNT, DRAFT_TOKENS, NS)
    c_vals = shared[:, NS:].reshape(REQUEST_COUNT, DRAFT_TOKENS, NS)
    head_gain = mixer_gain.reshape(MH, MP)

    def mamba_one(packed):
        return scan_one(packed[0], packed[1], packed[2], packed[3], packed[4], packed[5], decay_rate, skip_gain, head_gain)
    mamba = lax.map(mamba_one, (state_cache, inputs_x, gates_z, b_vals, c_vals, step_sizes))
    mixer_rows = jnp.concatenate([attention.reshape(ROWS, HEAD_GROUPS, query_size), mamba.reshape(ROWS, HEAD_GROUPS, m_size)], axis=2)
    summed = jnp.dot(mixer_rows.reshape(ROWS, HEAD_GROUPS * OCOL), mixer_out.reshape(HEAD_GROUPS * OCOL, D), preferred_element_type=jnp.float32)
    summed = summed + jnp.dot(hidden, down_weight, preferred_element_type=jnp.float32)
    return (rows_float + summed).astype(jnp.bfloat16)
```

```python
import functools
import jax
import jax.numpy as jnp
from jax import lax
from jax.experimental import pallas as pl
from jax.experimental.pallas import tpu as pltpu
from jax.sharding import PartitionSpec as P

D = 5120
QUERY_HEADS = 20
KEY_VALUE_HEADS = 4
HEAD_SIZE = 128
MH = 32
MP = 128
NS = 256
CACHE_SLOTS = 512
DRAFT_TOKENS = 4


epsilon = 1e-05


def as_sent(x):

    def short(part):
        return part.astype(jnp.bfloat16) if part.dtype == jnp.float32 else part

    return jax.tree.map(short, x)


def rotate(vectors, cos_table, sin_table):
    half_width = vectors.shape[-1] // 2
    first_half = vectors[..., :half_width]
    second_half = vectors[..., half_width:]
    return jnp.concatenate(
        [
            first_half * cos_table - second_half * sin_table,
            second_half * cos_table + first_half * sin_table,
        ],
        axis=-1,
    )


def rope_tables(positions):
    frequency = 10000.0 ** (-(jnp.arange(HEAD_SIZE // 2, dtype=jnp.float32) * 2.0 / HEAD_SIZE))
    angles = positions.astype(jnp.float32)[..., None] * frequency
    return (jnp.cos(angles), jnp.sin(angles))


def attend_one(queries, fresh_keys, fresh_values, key_tile_block, value_tile_block, length):
    score_scale = HEAD_SIZE ** (-0.5)
    scores_cache = (
        jnp.einsum("tkgd,pkd->kgtp", queries, key_tile_block, preferred_element_type=jnp.float32)
        * score_scale
    )
    scores_new = (
        jnp.einsum("tkgd,ukd->kgtu", queries, fresh_keys, preferred_element_type=jnp.float32)
        * score_scale
    )
    live_keys = jnp.arange(key_tile_block.shape[0], dtype=jnp.int32) < length
    causal = jnp.arange(DRAFT_TOKENS)[None, :] <= jnp.arange(DRAFT_TOKENS)[:, None]
    scores_cache = jnp.where(live_keys, scores_cache, -1e30)
    scores_new = jnp.where(causal, scores_new, -1e30)
    highest = jnp.maximum(jnp.max(scores_cache, axis=-1), jnp.max(scores_new, axis=-1))[..., None]
    weight_cache = jnp.exp(scores_cache - highest)
    weight_new = jnp.exp(scores_new - highest)
    denominator = jnp.sum(weight_cache, axis=-1, keepdims=True) + jnp.sum(
        weight_new, axis=-1, keepdims=True
    )
    probs_cache = (weight_cache / denominator).astype(jnp.bfloat16)
    probs_new = (weight_new / denominator).astype(jnp.bfloat16)
    attended = jnp.einsum(
        "kgtp,pkd->tkgd", probs_cache, value_tile_block, preferred_element_type=jnp.float32
    )
    attended = attended + jnp.einsum(
        "kgtu,ukd->tkgd", probs_new, fresh_values, preferred_element_type=jnp.float32
    )
    return attended.astype(jnp.bfloat16)


def scan_one(
    state_block, inputs_x, gates_z, b_vals, c_vals, step_sizes, decay_rates, skip_gain, head_gain
):
    hstate = state_block.astype(jnp.float32)
    in_active = jax.nn.silu(inputs_x.astype(jnp.float32))
    write_vec = jax.nn.silu(b_vals.astype(jnp.float32))
    read_vec = jax.nn.silu(c_vals.astype(jnp.float32))
    outputs = []
    for draft_index in range(DRAFT_TOKENS):
        decays = jnp.exp(-step_sizes[draft_index] * decay_rates)
        inject = (step_sizes[draft_index][:, None] * in_active[draft_index])[
            :, :, None
        ] * write_vec[draft_index][None, None, :]
        hstate = decays[:, None, None] * hstate + inject
        readout = jnp.einsum(
            "hpn,n->hp", hstate, read_vec[draft_index], precision=lax.Precision.HIGHEST
        )
        outputs.append(readout + skip_gain[:, None] * in_active[draft_index])
    gated = jnp.stack(outputs) * jax.nn.silu(gates_z.astype(jnp.float32))
    mean_square = jnp.mean(gated * gated, axis=-1, keepdims=True)
    return (gated * lax.rsqrt(mean_square + epsilon) * head_gain).astype(jnp.bfloat16)


def on_device(
    tokens,
    norm_gain,
    mixer_in,
    shared_in,
    step_in,
    step_bias,
    decay_rate,
    skip_gain,
    cached_keys,
    cached_values,
    lengths,
    state_cache,
    mixer_gain,
    mixer_out,
    gate_weight,
    up_weight,
    down_weight,
):
    short_count = lax.axis_size("short")
    n_wide = lax.axis_size("wide")
    q_heads = QUERY_HEADS // short_count
    key_value_heads = KEY_VALUE_HEADS // short_count
    ssm_heads = MH // short_count
    repeat_factor = QUERY_HEADS // KEY_VALUE_HEADS
    query_size = q_heads * HEAD_SIZE
    key_size = key_value_heads * HEAD_SIZE
    m_size = ssm_heads * MP
    local_rows = tokens.shape[0]
    requests = local_rows // DRAFT_TOKENS
    width_half = tokens.shape[1]
    rows_float = tokens.astype(jnp.float32)
    square_sum = lax.psum(jnp.sum(rows_float * rows_float, axis=1), "short")
    inv_rms = lax.rsqrt(square_sum / D + epsilon)
    normed = (rows_float * inv_rms[:, None] * norm_gain[None, :]).astype(jnp.bfloat16)
    step_terms = jnp.dot(normed, step_in, preferred_element_type=jnp.float32)
    step_raw = lax.psum_scatter(step_terms, "short", scatter_dimension=1, tiled=True)
    gathered = lax.all_gather(normed, "wide", axis=0, tiled=True)
    group_part = jnp.einsum("rd,dgc->rgc", gathered, mixer_in, preferred_element_type=jnp.float32)
    shared_part = jnp.dot(gathered, shared_in, preferred_element_type=jnp.float32)[:, None, :]
    gate_part = jnp.dot(gathered, gate_weight, preferred_element_type=jnp.float32)
    up_part = jnp.dot(gathered, up_weight, preferred_element_type=jnp.float32)
    gate_half, up_half = (
        lax.psum_scatter(
            gate_part.astype(jnp.bfloat16), "short", scatter_dimension=0, tiled=True
        ).astype(jnp.float32),
        lax.psum_scatter(
            up_part.astype(jnp.bfloat16), "short", scatter_dimension=0, tiled=True
        ).astype(jnp.float32),
    )
    hidden_half = (jax.nn.silu(gate_half) * up_half).astype(jnp.bfloat16)
    hidden = lax.all_gather(hidden_half, "short", axis=0, tiled=True)
    group_moved, shared_moved = (
        lax.all_to_all(group_part, "wide", split_axis=0, concat_axis=2, tiled=True),
        lax.all_to_all(shared_part, "wide", split_axis=0, concat_axis=2, tiled=True),
    )
    group_sum = lax.psum_scatter(group_moved, "short", scatter_dimension=1, tiled=True)
    shared_sum = lax.psum(shared_moved, "short")
    features = group_sum[:, 0, :].astype(jnp.bfloat16)
    shared_vals = shared_sum[:, 0, :].astype(jnp.bfloat16)
    queries = features[:, :query_size].reshape(requests, DRAFT_TOKENS, q_heads, HEAD_SIZE)
    fresh_keys = features[:, query_size : query_size + key_size].reshape(
        requests, DRAFT_TOKENS, key_value_heads, HEAD_SIZE
    )
    fresh_values = features[:, query_size + key_size : query_size + 2 * key_size].reshape(
        requests, DRAFT_TOKENS, key_value_heads, HEAD_SIZE
    )
    x_start = query_size + 2 * key_size
    inputs_x = features[:, x_start : x_start + m_size].reshape(
        requests, DRAFT_TOKENS, ssm_heads, MP
    )
    gates_z = features[:, x_start + m_size : x_start + 2 * m_size].reshape(
        requests, DRAFT_TOKENS, ssm_heads, MP
    )
    positions = lengths[:, None] + jnp.arange(DRAFT_TOKENS, dtype=jnp.int32)[None, :]
    cos_table, sin_table = rope_tables(positions)
    cos_table = cos_table[:, :, None, :]
    sin_table = sin_table[:, :, None, :]
    rotated_queries = rotate(queries.astype(jnp.float32), cos_table, sin_table).astype(jnp.bfloat16)
    keys_rot = rotate(fresh_keys.astype(jnp.float32), cos_table, sin_table).astype(jnp.bfloat16)
    rotated_queries = rotated_queries.reshape(
        requests, DRAFT_TOKENS, key_value_heads, repeat_factor, HEAD_SIZE
    )
    key_tile_block = cached_keys.reshape(requests, CACHE_SLOTS, key_value_heads, HEAD_SIZE)
    value_tile_block = cached_values.reshape(requests, CACHE_SLOTS, key_value_heads, HEAD_SIZE)
    attention = jax.vmap(attend_one)(
        rotated_queries, keys_rot, fresh_values, key_tile_block, value_tile_block, lengths
    )
    step_sizes = jax.nn.softplus(
        step_raw.reshape(requests, DRAFT_TOKENS, ssm_heads) + step_bias[None, None, :]
    )
    b_vals = shared_vals[:, :NS].reshape(requests, DRAFT_TOKENS, NS)
    c_vals = shared_vals[:, NS:].reshape(requests, DRAFT_TOKENS, NS)
    head_gain = mixer_gain.reshape(ssm_heads, MP)
    mamba = jax.vmap(scan_one, in_axes=(0, 0, 0, 0, 0, 0, None, None, None))(
        state_cache, inputs_x, gates_z, b_vals, c_vals, step_sizes, decay_rate, skip_gain, head_gain
    )
    own_rows = jnp.concatenate(
        [attention.reshape(local_rows, query_size), mamba.reshape(local_rows, m_size)], axis=1
    )
    returned = lax.all_to_all(
        as_sent(own_rows[:, None, :]), "wide", split_axis=2, concat_axis=0, tiled=True
    )
    both_groups = lax.all_gather(as_sent(returned), "short", axis=1, tiled=True).astype(
        returned.dtype
    )
    projected = jnp.einsum(
        "rgc,gcd->rd", both_groups, mixer_out, preferred_element_type=jnp.float32
    )
    summed = projected + jnp.dot(hidden, down_weight, preferred_element_type=jnp.float32)
    pieces = lax.all_to_all(
        summed.reshape(n_wide, local_rows, width_half).astype(jnp.bfloat16),
        "wide",
        split_axis=0,
        concat_axis=0,
        tiled=True,
    ).astype(jnp.float32)
    total = rows_float + jnp.sum(pieces, axis=0)
    return total.astype(jnp.bfloat16)


MESH = pl.DeviceIdType.MESH
F32 = jnp.float32
BF16 = jnp.bfloat16
NT = (((1,), (1,)), ((), ()))
LANE = 128


def silu(v):
    return v / (1.0 + jnp.exp(-v))


def dot(a, b):
    return jnp.dot(a, b, preferred_element_type=F32)


def dot_nt(a, b):
    return lax.dot_general(a, b, NT, preferred_element_type=F32)


def fused_kernel(
    dims,
    tokens, gain, bias, rate, skip, lengths, cosf, sinf, mixer_gain,
    mixer_in, shared_in, step_in, keys, values, state, mixer_out, gate, up, down,
    out,
    w_a, w_b, k_v, v_v, s_v, g_v, u_v, m_v, d_v,
    xg, xf, xb, sq_send, sq_recv, p_send, p_recv, c_b, tot, step_f,
    f_send, f_recv, feat, bc, qbuf, knbuf, vnbuf, obuf, cbuf, rbuf, own,
    m_send, m_recv, lhs, gsc, gu_send, gu_recv, hbuf, o_send, o_recv,
    sem_w, sem_loc, sem_gs, sem_gr, sem_ps, sem_pr, sem_fs, sem_fr,
    sem_ms, sem_mr, sem_us, sem_ur, sem_hs, sem_hr, sem_os, sem_or,
):
    n, n_short, rows, width, gcol, scol, ncol, ocol, n_chunk, fchunk, n_oc, ochunk = dims
    total_rows = n * rows
    me = lax.axis_index("wide")
    s = lax.axis_index("short")
    other = 1 - s
    q_heads = QUERY_HEADS // n_short
    kv_heads = KEY_VALUE_HEADS // n_short
    m_heads = MH // n_short
    rep = QUERY_HEADS // KEY_VALUE_HEADS
    acol = gcol + scol + ncol
    fpad = xpad(gcol)
    opad = round_up(ocol)

    def peer(d):
        return lax.rem(me + d, n)

    weights = []

    def fetch(src, dst):
        copy = pltpu.make_async_copy(src, dst, sem_w.at[len(weights)])
        copy.start()
        weights.append(copy)
        return copy

    fa = [
        fetch(mixer_in.at[other], w_a.at[pl.ds(0, gcol)]),
        fetch(shared_in, w_a.at[pl.ds(gcol, scol)]),
        fetch(step_in, w_a.at[pl.ds(gcol + scol, ncol)]),
    ]
    fb = [fetch(mixer_in.at[s], w_b)]

    barrier = pltpu.get_barrier_semaphore()
    for d in range(n):
        for e in range(n_short):
            if d or e:
                pl.semaphore_signal(
                    barrier, inc=1,
                    device_id={"wide": peer(d), "short": lax.rem(s + e, n_short)},
                    device_id_type=MESH,
                )

    def cols(c):
        return pl.ds(c * fchunk, fchunk)

    fgu = []
    for c in range(n_chunk):
        fgu.append((fetch(gate.at[:, cols(c)], g_v.at[c]), fetch(up.at[:, cols(c)], u_v.at[c])))
        if c == 0:
            fkv = [fetch(keys, k_v), fetch(values, v_v), fetch(state, s_v)]
    fmo = [fetch(mixer_out.at[g], m_v.at[g, pl.ds(0, ocol)]) for g in range(n_short)]
    fdn = [fetch(down.at[:, pl.ds(o * ochunk, ochunk)], d_v.at[o]) for o in range(n_oc)]

    pl.semaphore_wait(barrier, n * n_short - 1)

    def remote(src, dst, send, recv, wide, short):
        copy = pltpu.make_async_remote_copy(
            src_ref=src, dst_ref=dst, send_sem=send, recv_sem=recv,
            device_id={"wide": wide, "short": short}, device_id_type=MESH,
        )
        copy.start()
        return copy

    def arrived(buf, recv):
        pltpu.make_async_copy(buf, buf, recv).wait()

    sent = []

    for d in range(1, n):
        sent.append(remote(tokens, xg.at[me], sem_gs.at[d], sem_gr.at[me], peer(d), s))
    own_tokens = pltpu.make_async_copy(tokens, xg.at[me], sem_loc.at[0])
    own_tokens.start()
    for g in range(n_short):
        if opad > ocol:
            m_v[g, ocol:opad, :] = jnp.zeros((opad - ocol, width), BF16)
    feat[...] = jnp.zeros_like(feat)
    bc[...] = jnp.zeros_like(bc)
    qbuf[...] = jnp.zeros_like(qbuf)
    knbuf[...] = jnp.zeros_like(knbuf)
    vnbuf[...] = jnp.zeros_like(vnbuf)
    cbuf[...] = jnp.zeros_like(cbuf)
    c_b[...] = jnp.zeros_like(c_b)
    tot[...] = jnp.zeros_like(tot)
    own[...] = jnp.zeros_like(own)
    own_tokens.wait()
    for d in range(1, n):
        arrived(xg.at[peer(d)], sem_gr.at[peer(d)])
    for j in range(n):
        xf[rows * j : rows * (j + 1), :] = xg[j].astype(F32)
    x = xf[...]
    sq_send[...] = jnp.broadcast_to(jnp.sum(x * x, axis=1, keepdims=True), sq_send.shape)
    sent.append(remote(sq_send, sq_recv, sem_ps.at[0], sem_pr.at[0], me, other))
    xb[...] = (x * gain[...]).astype(BF16)

    for copy in fa:
        copy.wait()
    p_send[...] = dot_nt(xb[...], w_a[...])
    sent.append(remote(p_send, p_recv, sem_ps.at[1], sem_pr.at[1], me, other))
    fb[0].wait()
    c_b[:, :gcol] = dot_nt(xb[...], w_b[...])
    lane = lax.broadcasted_iota(jnp.int32, (total_rows, acol), 1)
    mine = jnp.where(lane < gcol, c_b[:, :acol], p_send[...])
    arrived(sq_recv, sem_pr.at[0])
    mean_square = (sq_send[:, :1] + sq_recv[:, :1]) / D
    inv = lax.rsqrt(mean_square + epsilon)
    arrived(p_recv, sem_pr.at[1])
    tot[:, :acol] = (mine + p_recv[...]) * inv
    whole = tot[...]
    wide_lane = lax.broadcasted_iota(jnp.int32, whole.shape, 1)
    span = whole.shape[1]
    features = pltpu.roll(
        jnp.where(wide_lane < gcol, whole, 0.0), lax.rem(me * gcol, LANE), 1
    )
    low = pltpu.roll(whole, span - gcol, 1)[:, :LANE]
    low_lane = lax.broadcasted_iota(jnp.int32, low.shape, 1)
    low = pltpu.roll(jnp.where(low_lane < scol, low, 0.0), lax.rem(me * scol, LANE), 1)
    step_all = pltpu.roll(whole, span - gcol - scol, 1)[:, :LANE]
    step_f[...] = pltpu.roll(step_all, lax.rem(LANE - s * m_heads, LANE), 1)
    tot[...] = features
    c_b[:, :LANE] = low
    for r in range(n):
        f_send[r, :, :fpad] = tot[rows * r : rows * (r + 1), :].astype(BF16)
        f_send[r, :, fpad:] = c_b[rows * r : rows * (r + 1), :LANE].astype(BF16)
    for d in range(1, n):
        to = peer(d)
        sent.append(remote(f_send.at[to], f_recv.at[me], sem_fs.at[d], sem_fr.at[me], to, s))
    own_f = pltpu.make_async_copy(f_send.at[me], f_recv.at[me], sem_loc.at[1])
    own_f.start()

    half = total_rows // n_short

    def gate_up(c):
        fgu[c][0].wait()
        for i in range(n_short):
            pass
        both = [dot(xb[...], g_v[c])]
        fgu[c][1].wait()
        both.append(dot(xb[...], u_v[c]))
        for k in range(2):
            for i in range(n_short):
                gsc[c, k, i] = both[k][half * i : half * (i + 1)] * inv[half * i : half * (i + 1)]
        for k in range(2):
            gu_send[c, k] = gsc[c, k, other].astype(BF16)
        sent.append(remote(gu_send.at[c], gu_recv.at[c], sem_us.at[c], sem_ur.at[c], me, other))

    def hidden(c):
        arrived(gu_recv.at[c], sem_ur.at[c])
        a = gsc[c, 0, s] + gu_recv[c, 0].astype(F32)
        b = gsc[c, 1, s] + gu_recv[c, 1].astype(F32)
        hbuf[c, s] = (silu(a) * b).astype(BF16)
        sent.append(
            remote(hbuf.at[c, s], hbuf.at[c, s], sem_hs.at[c], sem_hr.at[c], me, other)
        )

    gate_up(0)

    own_f.wait()
    for d in range(1, n):
        arrived(f_recv.at[peer(d)], sem_fr.at[peer(d)])
    fwidth = feat.shape[1]
    for j in range(n):
        base = gcol * j // LANE * LANE
        w = min(fpad, fwidth - base)
        feat[:, base : base + w] += f_recv[j, :, :w].astype(F32)
        base = scol * j // LANE * LANE
        bc[:, base : base + LANE] += f_recv[j, :, fpad:].astype(F32)
    for copy in fkv:
        copy.wait()
    k_at = q_heads * HEAD_SIZE
    v_at = k_at + kv_heads * HEAD_SIZE
    x_at = v_at + kv_heads * HEAD_SIZE
    z_at = x_at + m_heads * MP
    cos_t = cosf[...]
    sin_t = sinf[...]

    def turn(v):
        return v * cos_t + jnp.concatenate([v[:, HEAD_SIZE // 2 :], v[:, : HEAD_SIZE // 2]], axis=1) * sin_t

    length = lengths[0]
    for kv in range(kv_heads):
        for i in range(rep):
            h = kv * rep + i
            qbuf[kv, rows * i : rows * (i + 1), :] = turn(feat[:, h * HEAD_SIZE : (h + 1) * HEAD_SIZE])
        knbuf[kv, :rows, :] = turn(feat[:, k_at + kv * HEAD_SIZE : k_at + (kv + 1) * HEAD_SIZE])
        vnbuf[kv, :rows, :] = feat[:, v_at + kv * HEAD_SIZE : v_at + (kv + 1) * HEAD_SIZE]
        head = slice(kv * HEAD_SIZE, (kv + 1) * HEAD_SIZE)
        query = qbuf[kv].astype(BF16)
        scale = HEAD_SIZE ** (-0.5)
        old = dot_nt(query, k_v[:, head]) * scale
        new = dot_nt(query, knbuf[kv].astype(BF16)) * scale
        slot = lax.broadcasted_iota(jnp.int32, old.shape, 1)
        old = jnp.where(slot < length, old, -1e30)
        token = lax.rem(lax.broadcasted_iota(jnp.int32, new.shape, 0), rows)
        fresh = lax.broadcasted_iota(jnp.int32, new.shape, 1)
        new = jnp.where(fresh <= token, new, -1e30)
        top = jnp.maximum(
            jnp.max(old, axis=1, keepdims=True), jnp.max(new, axis=1, keepdims=True)
        )
        old = jnp.exp(old - top)
        new = jnp.exp(new - top)
        den = jnp.sum(old, axis=1, keepdims=True) + jnp.sum(new, axis=1, keepdims=True)
        obuf[kv] = dot((old / den).astype(BF16), v_v[:, head]) + dot(
            (new / den).astype(BF16), vnbuf[kv].astype(BF16)
        )
        for i in range(rep):
            h = kv * rep + i
            own[:, h * HEAD_SIZE : (h + 1) * HEAD_SIZE] = obuf[kv, rows * i : rows * (i + 1), :]

    write = silu(bc[:, :NS])
    read = silu(bc[:, NS:])
    rest = read
    for i in range(3):
        piece = rest.astype(BF16).astype(F32)
        cbuf[rows * i : rows * (i + 1), :] = piece
        rest = rest - piece
    rbuf[...] = dot_nt(cbuf[...].astype(BF16), s_v[...])
    carried = rbuf[:rows] + rbuf[rows : 2 * rows] + rbuf[2 * rows : 3 * rows]
    raw = step_f[pl.ds(rows * me, rows), :][:, :m_heads] + bias[...]
    step = jnp.maximum(raw, 0.0) + jnp.log1p(jnp.exp(-jnp.abs(raw)))
    run = [step[:1]]
    for t in range(1, rows):
        run.append(run[-1] + step[t : t + 1])
    age = jnp.concatenate(run, axis=0) * rate[...]
    kept = jnp.exp(-age)
    tid = lax.broadcasted_iota(jnp.int32, age.shape, 0)
    mix = []
    for u in range(rows):
        overlap = jnp.sum(read * write[u : u + 1], axis=1, keepdims=True)
        fade = jnp.exp(-jnp.maximum(age - age[u : u + 1], 0.0))
        mix.append(jnp.where(tid >= u, fade, 0.0) * step[u : u + 1] * overlap)
    skips = skip[...]
    for h in range(m_heads):
        hs = slice(h * MP, (h + 1) * MP)
        active = silu(feat[:, x_at + h * MP : x_at + (h + 1) * MP])
        y = kept[:, h : h + 1] * carried[:, hs] + skips[:, h : h + 1] * active
        for u in range(rows):
            y = y + mix[u][:, h : h + 1] * active[u : u + 1]
        y = y * silu(feat[:, z_at + h * MP : z_at + (h + 1) * MP])
        ms = jnp.mean(y * y, axis=1, keepdims=True)
        at = (q_heads + h) * MP
        own[:, at : at + MP] = y * lax.rsqrt(ms + epsilon) * mixer_gain[:, hs]

    window = opad + LANE
    for j in range(n):
        base = ocol * j // LANE * LANE
        off = ocol * j - base
        v = own[:, base : base + window]
        if off:
            v = jnp.concatenate([v[:, off:], v[:, :off]], axis=1)
        m_send[j] = v[:, :opad].astype(BF16)
    for d in range(n):
        to = peer(d)
        for e in range(n_short):
            if d or e:
                sent.append(
                    remote(
                        m_send.at[to], m_recv.at[s, me], sem_ms.at[d, e], sem_mr.at[s, me],
                        to, lax.rem(s + e, n_short),
                    )
                )
    own_m = pltpu.make_async_copy(m_send.at[me], m_recv.at[s, me], sem_loc.at[2])
    own_m.start()

    hidden(0)
    for c in range(1, n_chunk):
        gate_up(c)
        if c > 1:
            hidden(c - 1)
    own_m.wait()
    for d in range(n):
        for e in range(n_short):
            if d or e:
                g = lax.rem(s + e, n_short)
                arrived(m_recv.at[g, peer(d)], sem_mr.at[g, peer(d)])
    for g in range(n_short):
        for j in range(n):
            lhs[g, rows * j : rows * (j + 1), :] = m_recv[g, j].astype(F32)
    if n_chunk > 1:
        hidden(n_chunk - 1)
    for copy in fmo:
        copy.wait()
    for c in range(n_chunk):
        arrived(hbuf.at[c, other], sem_hr.at[c])
    for o in range(n_oc):
        oc = slice(o * ochunk, (o + 1) * ochunk)
        acc = dot(lhs[0].astype(BF16), m_v[0, :, oc])
        for g in range(1, n_short):
            acc = acc + dot(lhs[g].astype(BF16), m_v[g, :, oc])
        fdn[o].wait()
        for c in range(n_chunk):
            acc = acc + dot(
                hbuf[c].reshape(total_rows, fchunk), d_v[o, c * fchunk : (c + 1) * fchunk, :]
            )
        xf[:, oc] = acc
        for r in range(n):
            o_send[o, r] = xf[rows * r : rows * (r + 1), oc].astype(BF16)
        for d in range(1, n):
            to = peer(d)
            sent.append(
                remote(
                    o_send.at[o, to], o_recv.at[o, me], sem_os.at[o, d], sem_or.at[o, me], to, s
                )
            )
    for o in range(n_oc):
        oc = slice(o * ochunk, (o + 1) * ochunk)
        acc = tokens[:, oc].astype(F32) + o_send[o, me].astype(F32)
        for d in range(1, n):
            arrived(o_recv.at[o, peer(d)], sem_or.at[o, peer(d)])
            acc = acc + o_recv[o, peer(d)].astype(F32)
        out[:, oc] = acc.astype(BF16)
    for copy in sent:
        copy.wait_send()


def round_up(v):
    return -(-v // LANE) * LANE


def xpad(gcol):
    return round_up(gcol + LANE - 1)


def pieces_of(width, most):
    tiles = width // LANE
    for k in range(most, 0, -1):
        if tiles % k == 0:
            return k
    return 1


def fused(*args):
    (tokens, norm_gain, mixer_in, shared_in, step_in, step_bias, decay_rate, skip_gain,
     cached_keys, cached_values, lengths, state_cache, mixer_gain, mixer_out,
     gate_weight, up_weight, down_weight) = args
    n = lax.axis_size("wide")
    n_short = lax.axis_size("short")
    rows, width = tokens.shape
    gcol = mixer_in.shape[2]
    scol = shared_in.shape[1]
    ncol = step_in.shape[1]
    ocol = mixer_out.shape[1]
    ffl = gate_weight.shape[1]
    n_chunk = pieces_of(ffl, 3)
    fchunk = ffl // n_chunk
    n_oc = pieces_of(width, 4)
    ochunk = width // n_oc
    m_heads = MH // n_short
    kv_heads = KEY_VALUE_HEADS // n_short
    total_rows = n * rows
    acol = gcol + scol + ncol
    fpad = xpad(gcol)
    opad = round_up(ocol)
    features = n * gcol
    outs = n * ocol
    half = total_rows // n_short
    positions = lengths + jnp.arange(rows, dtype=jnp.int32)
    cos_table, sin_table = rope_tables(positions)
    cosf = jnp.concatenate([cos_table, cos_table], axis=-1)
    sinf = jnp.concatenate([-sin_table, sin_table], axis=-1)
    dims = (n, n_short, rows, width, gcol, scol, ncol, ocol, n_chunk, fchunk, n_oc, ochunk)
    vm = pl.BlockSpec(memory_space=pltpu.VMEM)
    sm = pl.BlockSpec(memory_space=pltpu.SMEM)
    hb = pl.BlockSpec(memory_space=pl.ANY)
    V = pltpu.VMEM
    dma = pltpu.SemaphoreType.DMA
    kvw = cached_keys.shape[2]
    slots = cached_keys.shape[1]
    scratch = [
        V((acol, width), BF16), V((gcol, width), BF16), V((slots, kvw), BF16),
        V((slots, kvw), BF16), V((m_heads * MP, NS), BF16),
        V((n_chunk, width, fchunk), BF16), V((n_chunk, width, fchunk), BF16),
        V((n_short, opad, width), BF16), V((n_oc, ffl, ochunk), BF16),
        V((n, rows, width), BF16), V((total_rows, width), F32), V((total_rows, width), BF16),
        V((total_rows, LANE), F32), V((total_rows, LANE), F32),
        V((total_rows, acol), F32), V((total_rows, acol), F32), V((total_rows, fpad), F32),
        V((total_rows, fpad), F32), V((total_rows, LANE), F32),
        V((n, rows, fpad + LANE), BF16), V((n, rows, fpad + LANE), BF16),
        V((rows, features), F32), V((rows, 2 * NS), F32),
        V((kv_heads, 32, HEAD_SIZE), F32), V((kv_heads, 16, HEAD_SIZE), F32),
        V((kv_heads, 16, HEAD_SIZE), F32), V((kv_heads, 32, HEAD_SIZE), F32),
        V((16, NS), F32), V((16, m_heads * MP), F32),
        V((rows, round_up(outs) + opad + LANE), F32),
        V((n, rows, opad), BF16), V((n_short, n, rows, opad), BF16),
        V((n_short, total_rows, opad), F32),
        V((n_chunk, 2, n_short, half, fchunk), F32),
        V((n_chunk, 2, half, fchunk), BF16), V((n_chunk, 2, half, fchunk), BF16),
        V((n_chunk, n_short, half, fchunk), BF16),
        V((n_oc, n, rows, ochunk), BF16), V((n_oc, n, rows, ochunk), BF16),
        dma((4 + 2 * n_chunk + 3 + n_short + n_oc,)), dma((3,)),
        dma((n,)), dma((n,)), dma((2,)), dma((2,)), dma((n,)), dma((n,)),
        dma((n, n_short)), dma((n_short, n)), dma((n_chunk,)), dma((n_chunk,)),
        dma((n_chunk,)), dma((n_chunk,)), dma((n_oc, n)), dma((n_oc, n)),
    ]
    return pl.pallas_call(
        functools.partial(fused_kernel, dims),
        out_shape=jax.ShapeDtypeStruct((rows, width), BF16),
        in_specs=[vm, vm, vm, vm, vm, sm, vm, vm, vm] + [hb] * 10,
        out_specs=vm,
        scratch_shapes=scratch,
        name="layer",
        compiler_params=pltpu.CompilerParams(
            collective_id=0, has_side_effects=True, vmem_limit_bytes=66 * 1000 * 1000
        ),
    )(
        tokens, norm_gain[None, :], step_bias[None, :], decay_rate[None, :], skip_gain[None, :],
        lengths, cosf, sinf, mixer_gain[None, :],
        jnp.transpose(mixer_in, (1, 2, 0)), shared_in.T, step_in.T,
        cached_keys[0], cached_values[0], state_cache.reshape(m_heads * MP, NS),
        mixer_out, gate_weight, up_weight, down_weight,
    )


def fits(n, n_short, args):
    tokens, mixer_in, shared_in, step_in = args[0], args[2], args[3], args[4]
    return (
        n_short == 2
        and tokens.shape[0] == DRAFT_TOKENS
        and n * DRAFT_TOKENS == 32
        and mixer_in.shape[2] % 16 == 0
        and shared_in.shape[1] % 16 == 0
        and LANE % shared_in.shape[1] == 0
        and step_in.shape[1] % 16 == 0
        and args[13].shape[1] % 16 == 0
        and args[14].shape[1] % LANE == 0
    )


def layer(*args):
    if fits(lax.axis_size("wide"), lax.axis_size("short"), args):
        return fused(*args)
    return on_device(*args)


def solution(mesh):
    in_specs = (
        P(("groups", "wide"), "short"),
        P("short"),
        P("short", None, "wide"),
        P("short", "wide"),
        P("short", None),
        P("short"),
        P("short"),
        P("short"),
        P(("groups", "wide"), None, "short"),
        P(("groups", "wide"), None, "short"),
        P(("groups", "wide")),
        P(("groups", "wide"), "short", None, None),
        P("short"),
        P(None, "wide", "short"),
        P("short", "wide"),
        P("short", "wide"),
        P("wide", "short"),
    )
    out_specs = P(("groups", "wide"), "short")
    return jax.shard_map(
        layer, mesh=mesh, in_specs=in_specs, out_specs=out_specs, check_vma=False
    )
```
